32 devices in a mesh: seq: 8 (over z, core), expert: 4 (over y, x).
Axes of the slice: x: 2, y: 2, z: 4, core: 2. Of those that a mesh axis runs over, the one named last changes fastest.
Arguments:
- tokens: bfloat16 [4, 32, 4096], P('expert', 'seq'), may hold values from -6 to 6
- out_grad: bfloat16 [4, 32, 4096], P('expert', 'seq'), may hold values from -12 to 12
- expert_ids: int32 [4, 32, 8], P('expert', 'seq'), may hold values from 0 to 15, as said below
- route_gates: bfloat16 [4, 32, 8], P('expert', 'seq'), may hold values from 0.019897461 to 0.5
- gate_weight: bfloat16 [16, 1536, 4096], P('expert', 'seq'), may hold values from -0.09375 to 0.09375
- up_weight: bfloat16 [16, 1536, 4096], P('expert', 'seq'), may hold values from -0.09375 to 0.09375
- down_weight: bfloat16 [16, 1536, 4096], P('expert', 'seq'), may hold values from -0.15625 to 0.15625
Outputs:
- token_grad: bfloat16 [4, 32, 4096], P('expert', 'seq')
The draws below stay inside these ranges and needn't reach their ends.
Inputs may be any that keep to these rules, and one draw needn't show every extreme that they name: `expert_ids`: each token names 8 different experts; within each index of the first dimension (one group of 32 tokens) every expert is named at most 32 times, and some expert exactly 32 times.
All inputs are finite; a program needn't handle non-finite values.
Results may differ from the reference program's by a relative error of at most 0.0057.
Values may be sent and summed in bfloat16 or wider, within the bound.
No kernel may reach another device: no remote copies, remote signals or barrier semaphores. Data moves between devices by JAX's collectives and lax.ppermute only.
A program may use at most 128 MiB of HBM per device.

```python
import math
import jax
import jax.numpy as jnp
from jax import lax

D = 4096
FF = 1536
TOPK = 8
EXP_DEV = 4
E = 16
GROUPS = 4
GROUP_TOK = 32
CAP = 32
N_SEQ = 8


def group_ids(group_key, hot_device):
    order_key, delta_key, perm_key, roll_key = jax.random.split(group_key, 4)
    mean_load = CAP // 2
    device_of = jnp.arange(E, dtype=jnp.int32) // EXP_DEV
    shuffled = jax.random.permutation(order_key, E).astype(jnp.int32)
    scores = jnp.where(device_of == hot_device, jnp.arange(E, dtype=jnp.int32) - E, shuffled)
    rank_order = jnp.argsort(scores, stable=True).astype(jnp.int32)
    rest_count = E - 2 * EXP_DEV
    load_delta = jax.random.randint(delta_key, (rest_count // 2,), -mean_load, mean_load + 1)
    rest_loads = jnp.stack([mean_load + load_delta, mean_load - load_delta], axis=1).reshape(-1)
    by_rank = jnp.concatenate([jnp.full((EXP_DEV,), CAP, jnp.int32), jnp.zeros((EXP_DEV,), jnp.int32), rest_loads.astype(jnp.int32)])
    expert_loads = jnp.zeros((E,), jnp.int32).at[rank_order].set(by_rank)
    load_ends = jnp.cumsum(expert_loads)
    slot_ids = jnp.arange(GROUP_TOK * TOPK, dtype=jnp.int32)
    labels = jnp.sum((load_ends[None, :] <= slot_ids[:, None]).astype(jnp.int32), axis=1)
    id_table = labels.reshape(TOPK, GROUP_TOK).T
    id_table = id_table[jax.random.permutation(perm_key, GROUP_TOK)]
    col_shift = jax.random.randint(roll_key, (GROUP_TOK, 1), 0, TOPK)
    columns = (jnp.arange(TOPK, dtype=jnp.int32)[None, :] + col_shift) % TOPK
    return jnp.take_along_axis(id_table, columns, axis=1).astype(jnp.int32)


def draw_expert_ids(key, part):
    hot_device = jax.random.randint(jax.random.fold_in(key, 7), (), 0, E // EXP_DEV)
    group_keys = jax.random.split(jax.random.fold_in(key, 11), GROUPS)

    def one_group(group_key):
        return group_ids(group_key, hot_device)
    return jax.vmap(one_group)(group_keys)


def steps_of(key, dims, cuts, smallest, high):
    gain, own = 1.0, jax.random.fold_in(key, 6)
    for axis_at, shards_of in cuts:
        heights = jnp.exp(jax.random.uniform(jax.random.fold_in(own, axis_at), (shards_of,), jnp.float32, smallest / len(cuts), high / len(cuts)))
        gain = gain * jnp.repeat(heights, dims[axis_at] // shards_of).reshape([-1 if axis == axis_at else 1 for axis in range(len(dims))])
    return gain


def centred(own_key, dims, scale, reach, cuts=(), held_as=jnp.bfloat16):
    gain = steps_of(own_key, dims, cuts, -0.22, 0.18) if cuts else 1.0
    array = jax.random.normal(own_key, dims, jnp.float32) * scale * gain
    return jnp.minimum(jnp.maximum(array, -reach), reach).astype(held_as)


def setup_inputs(seed: int = 0) -> dict:
    arg_keys = jax.random.split(jax.random.key(seed), 8)
    return {
        "tokens": centred(arg_keys[0], (GROUPS, GROUP_TOK, D), 1.0, 6.0, ((0, 4), (1, 8))),
        "out_grad": centred(arg_keys[1], (GROUPS, GROUP_TOK, D), 2.0, 12.0, ((0, 4), (1, 8))),
        "expert_ids": draw_expert_ids(jax.random.fold_in(arg_keys[7], 71), 0),
        "route_gates": jnp.clip(jnp.exp(math.log(0.5) - 3.224016 * jax.random.uniform(arg_keys[3], (GROUPS, GROUP_TOK, TOPK), jnp.float32) ** steps_of(arg_keys[3], (GROUPS, GROUP_TOK, TOPK), ((0, 4), (1, 8)), -0.2, 0.2)), 0.019897461, 0.5).astype(jnp.bfloat16),
        "gate_weight": centred(arg_keys[4], (E, FF, D), D ** -0.5, 0.09375, ((0, 4), (1, 8))),
        "up_weight": centred(arg_keys[5], (E, FF, D), D ** -0.5, 0.09375, ((0, 4), (1, 8))),
        "down_weight": centred(arg_keys[6], (E, FF, D), FF ** -0.5, 0.15625, ((0, 4), (1, 8))),
    }


def swiglu_back(gate_act, up_act, hidden_grad):
    sigmoid = jax.nn.sigmoid(gate_act)
    d_gate = (hidden_grad * up_act * sigmoid * (1.0 + gate_act * (1.0 - sigmoid))).astype(jnp.bfloat16)
    d_up = (hidden_grad * gate_act * sigmoid).astype(jnp.bfloat16)
    return d_gate, d_up


def reference(tokens, out_grad, expert_ids, route_gates, gate_weight, up_weight, down_weight):
    model_width = tokens.shape[2]
    flat_input = tokens.reshape(-1, model_width)
    flat_grad = out_grad.reshape(-1, model_width)
    count_tok = flat_input.shape[0]
    top_count = expert_ids.shape[2]
    experts = gate_weight.shape[0]
    hidden = gate_weight.shape[1]
    per_range = hidden // N_SEQ
    most_rows = GROUPS * CAP
    flat_ids = expert_ids.reshape(-1).astype(jnp.int32)
    onehot = (flat_ids[:, None] == jnp.arange(experts, dtype=jnp.int32)[None, :]).astype(jnp.int32)
    position = jnp.sum(jnp.cumsum(onehot, axis=0) * onehot, axis=1) - 1
    slot_index = (flat_ids * most_rows + position).astype(jnp.int32)
    route_token = (jnp.arange(flat_ids.shape[0], dtype=jnp.int32) // top_count).astype(jnp.int32)
    slot_token = jnp.full((experts * most_rows,), count_tok, jnp.int32).at[slot_index].set(route_token)
    slot_token = slot_token.reshape(experts, most_rows)
    slot_gate = jnp.zeros((experts * most_rows,), jnp.float32).at[slot_index].set(
        route_gates.reshape(-1).astype(jnp.float32)).reshape(experts, most_rows)
    padded_input = jnp.concatenate([flat_input, jnp.zeros((1, model_width), flat_input.dtype)], axis=0)
    padded_grad = jnp.concatenate([flat_grad, jnp.zeros((1, model_width), flat_grad.dtype)], axis=0)

    def one_expert(summed, inputs):
        gate_mat, up_mat, down_mat, token_rows, gate_rows = inputs
        input_rows = jnp.take(padded_input, token_rows, axis=0)
        grad_rows = jnp.take(padded_grad, token_rows, axis=0)
        gate_act = jnp.dot(input_rows, gate_mat.T, preferred_element_type=jnp.float32)
        up_act = jnp.dot(input_rows, up_mat.T, preferred_element_type=jnp.float32)
        down_back = jnp.dot(grad_rows, down_mat.T, preferred_element_type=jnp.float32)
        d_gate, d_up = swiglu_back(gate_act, up_act, down_back * gate_rows[:, None])
        range_gate = jnp.einsum('rsf,sfd->rsd',
                                d_gate.reshape(-1, N_SEQ, per_range).astype(jnp.float32),
                                gate_mat.reshape(N_SEQ, per_range, model_width).astype(jnp.float32))
        range_up = jnp.einsum('rsf,sfd->rsd',
                              d_up.reshape(-1, N_SEQ, per_range).astype(jnp.float32),
                              up_mat.reshape(N_SEQ, per_range, model_width).astype(jnp.float32))
        rounded = (range_gate + range_up).astype(jnp.bfloat16)
        rounded = lax.optimization_barrier(rounded)
        row_sums = jnp.sum(rounded.astype(jnp.float32), axis=1)
        return summed.at[token_rows].add(row_sums), None

    start_sum = jnp.zeros((count_tok + 1, model_width), jnp.float32)
    summed, _unused = lax.scan(one_expert, start_sum,
                               (gate_weight, up_weight, down_weight, slot_token, slot_gate))
    return summed[:count_tok].astype(jnp.bfloat16).reshape(tokens.shape)
```

```python
import jax
import jax.numpy as jnp
from jax import lax
from jax.sharding import Mesh, PartitionSpec as P

LANES = 128


def physical_mesh(mesh):
    devices = mesh.devices
    cores = len({d.core_on_chip for d in devices.flat})
    size_x = len({d.coords[0] for d in devices.flat})
    seq, expert = devices.shape
    shape = (seq // cores, cores, expert // size_x, size_x)
    return Mesh(devices.reshape(shape), ("z", "c", "y", "x"))


def swap_pairs(sizes, flip):
    cores, size_y, size_x = sizes
    flat = lambda c, y, x: (c * size_y + y) * size_x + x
    return [
        (flat(c, y, x), flat(*flip(c, y, x)))
        for c in range(cores)
        for y in range(size_y)
        for x in range(size_x)
    ]


def dense_gates(ids, gates, width):
    lane = lax.broadcasted_iota(jnp.int32, (1, 1, width), 2)
    hit = ids[:, :, None] == lane
    return jnp.sum(jnp.where(hit, gates[:, :, None].astype(jnp.float32), 0.0), axis=1).astype(jnp.bfloat16)


def per_device(sizes, tokens, out_grad, expert_ids, route_gates, gate_weight, up_weight, down_weight):
    size_z, cores, size_y, size_x = sizes
    x, dy, ids, gates = tokens[0], out_grad[0], expert_ids[0], route_gates[0]
    count, width = x.shape
    local, hidden, _ = gate_weight.shape
    experts = local * size_y * size_x
    pad = -(-experts // LANES) * LANES
    core = lax.axis_index("c")
    first = core == 0
    trio = ("c", "y", "x")
    swap = [(0, 1), (1, 0)]
    near = [
        swap_pairs((cores, size_y, size_x), lambda c, y, x, k=k: (c, y, x ^ k) if c == 0 else (c, y ^ k, x))
        for k in range(1, size_x)
    ]
    far = [
        swap_pairs((cores, size_y, size_x), lambda c, y, x, k=k: (c, y ^ k, x) if c == 0 else (c, y, x ^ k))
        for k in range(1, size_x)
    ]
    column = [[(z, z ^ k) for z in range(size_z)] for k in range(1, size_z)]

    dense = dense_gates(ids, gates, pad)
    xg = jnp.concatenate([x, dense], axis=1)
    dg = jnp.concatenate([dy, jnp.zeros_like(dense)], axis=1)
    keep, send = jnp.where(first, xg, dg), jnp.where(first, dg, xg)
    got = lax.ppermute(send, "c", swap)
    block = jnp.concatenate([jnp.where(first, keep, got), jnp.where(first, got, keep)], axis=0)
    block = jnp.concatenate([block] + [lax.ppermute(block, "z", p) for p in column], axis=0)
    block = jnp.concatenate([block] + [lax.ppermute(block, trio, p) for p in near], axis=0)
    block = jnp.concatenate([block] + [lax.ppermute(block, trio, p) for p in far], axis=0)
    other = lax.ppermute(block, "c", swap)
    rows = block.shape[0]
    unit = rows // (size_x * size_y)
    turn = lambda a: a.reshape(size_x, size_x, -1, a.shape[-1]).swapaxes(0, 1).reshape(a.shape)
    other = turn(other)
    all_x = jnp.where(first, block, other)
    all_dy = jnp.where(first, other, block)[:, :width]
    all_gates = all_x[:, width:]
    all_x = all_x[:, :width]

    me = lax.axis_index(("y", "x"))
    gate_mat, up_mat, down_mat = (
        w.reshape(local * hidden, width) for w in (gate_weight, up_weight, down_weight)
    )
    owner = me * local + lax.broadcasted_iota(jnp.int32, (pad, local * hidden), 1) // hidden
    spread = (lax.broadcasted_iota(jnp.int32, (pad, local * hidden), 0) == owner).astype(jnp.bfloat16)
    dot_t = lambda a, w: lax.dot_general(a, w, (((1,), (1,)), ((), ())), preferred_element_type=jnp.float32)
    gate_act = dot_t(all_x, gate_mat)
    up_act = dot_t(all_x, up_mat)
    down_back = dot_t(all_dy, down_mat)
    weight = jnp.dot(all_gates, spread, preferred_element_type=jnp.float32)
    hidden_grad = down_back * weight
    sigmoid = jax.nn.sigmoid(gate_act)
    d_gate = (hidden_grad * up_act * sigmoid * (1.0 + gate_act * (1.0 - sigmoid))).astype(jnp.bfloat16)
    d_up = (hidden_grad * gate_act * sigmoid).astype(jnp.bfloat16)
    pick = lambda d: d.reshape(-1, cores, count, d.shape[-1]).swapaxes(0, 1).reshape(d.shape)
    d_gate, d_up = pick(d_gate), pick(d_up)
    part = jnp.dot(d_gate, gate_mat, preferred_element_type=jnp.float32)
    part = part + jnp.dot(d_up, up_mat, preferred_element_type=jnp.float32)
    half = rows // cores
    mine = jnp.where(first, part[:half], part[half:])
    away = jnp.where(first, part[half:], part[:half]).astype(jnp.bfloat16)
    mine = mine + turn(lax.ppermute(away, "c", swap)).astype(jnp.float32)

    def reduce_over(mine, axes, moves):
        n = len(moves) + 1
        parts = mine.reshape(n, -1, mine.shape[-1])
        total = parts[0]
        for k, pairs in enumerate(moves, 1):
            total = total + lax.ppermute(parts[k].astype(jnp.bfloat16), axes, pairs).astype(jnp.float32)
        return total

    mine = reduce_over(mine, trio, far)
    mine = reduce_over(mine, trio, near)
    mine = reduce_over(mine, "z", column)
    return mine.astype(jnp.bfloat16)[None]


def solution(mesh):
    phys = physical_mesh(mesh)
    sizes = tuple(phys.shape[n] for n in ("z", "c", "y", "x"))
    spec = P(("y", "x"), ("z", "c"), None)

    def step(*args):
        return per_device(sizes, *args)

    return jax.shard_map(step, mesh=phys, in_specs=(spec,) * 7, out_specs=spec, check_vma=False)
```
